32 devices in a mesh: mom: 8 (over z, x), row: 2 (over core), col: 2 (over y).
Axes of the slice: x: 2, y: 2, z: 4, core: 2. Of those that a mesh axis runs over, the one named last changes fastest.
Arguments:
- left_part: bfloat16 [8, 1536, 1536], P('mom', 'row', 'col'), may hold values from -0.15625 to 0.15625
- vertex: bfloat16 [8, 1536, 1536], P('mom', 'row', 'col'), may hold values from -6 to 6
- bubble: float32 [8, 1536], P('mom'), may hold values from 0.25 to 2
- cross_map: int32 [1536, 8], P(('col', 'mom')), may hold values from 0 to 7, each once within a row
Outputs:
- crossed: bfloat16 [1536, 8, 1536], P(('col', 'mom'), None, 'row')
The draws below stay inside these ranges and needn't reach their ends.
Inputs may be any that keep to these rules, and one draw needn't show every extreme that they name: Each row cross_map[b, :] is a permutation of the 8 transfer momenta.
All inputs are finite; a program needn't handle non-finite values.
Results may differ from the reference program's by a relative error of at most 0.0055.
Values may be sent and summed in bfloat16 or wider, within the bound.
No kernel may reach another device: no remote copies, remote signals or barrier semaphores. Data moves between devices by JAX's collectives and lax.ppermute only.
A program may use at most 64 MiB of HBM per device.

```python
import jax
import jax.numpy as jnp
from jax import lax

M = 1536
NQ = 8


def block_levels(rng, extent, cuts, smallest, top_value):
    def one(position, parts):
        draws = jax.random.uniform(jax.random.fold_in(jax.random.fold_in(rng, 6), position), (parts,), jnp.float32, smallest / len(cuts), top_value / len(cuts))
        return jnp.repeat(jnp.exp(draws), extent[position] // parts).reshape((-1,) + (1,) * (len(extent) - position - 1))

    loudness = one(*cuts[0])
    for cut in cuts[1:]:
        loudness = loudness * one(*cut)
    return loudness


def gaussian(own_key, extent, scale, most, shards=(), kind=jnp.bfloat16):
    values = scale * jax.random.normal(own_key, extent, jnp.float32)
    if shards:
        values = values * block_levels(own_key, extent, shards, -0.22, 0.18)
    return jnp.clip(values, -most, most).astype(kind)


def setup_inputs(seed: int = 0) -> dict:
    key_of = jax.random.split(jax.random.key(seed), 5)
    return {
        "left_part": gaussian(key_of[0], (NQ, M, M), M ** -0.5, 0.15625, ((0, 8), (1, 2), (2, 2))),
        "vertex": gaussian(key_of[1], (NQ, M, M), 1.0, 6.0, ((0, 8), (1, 2), (2, 2))),
        "bubble": jnp.clip(0.25 + 1.75 * jax.random.uniform(key_of[2], (NQ, M), jnp.float32) ** block_levels(key_of[2], (NQ, M), ((0, 8),), -0.2, 0.2), 0.25, 2.0),
        "cross_map": jax.vmap(lambda own: jax.random.permutation(own, NQ))(jax.random.split(key_of[3], M)).reshape((M, NQ)).astype(jnp.int32),
    }


def one_momentum(operands):
    left_part, vertex, bubble = operands
    weighted = (left_part.astype(jnp.float32) * bubble[None, :]).astype(jnp.bfloat16)
    first = jnp.dot(weighted, vertex, preferred_element_type=jnp.float32)
    first_round = first.astype(jnp.bfloat16)
    second = jnp.dot(weighted, first_round, preferred_element_type=jnp.float32)
    return (vertex.astype(jnp.float32) + first + second).astype(jnp.bfloat16)


def reference(left_part, vertex, bubble, cross_map):
    corrected = lax.map(one_momentum, (left_part, vertex, bubble))

    def cross_column(operands):
        column, mapping = operands
        return corrected[mapping, :, column]

    columns = jnp.arange(M, dtype=jnp.int32)
    return lax.map(cross_column, (columns, cross_map.astype(jnp.int32)))
```

```python
import jax
import jax.numpy as jnp
from jax import lax
from jax.sharding import PartitionSpec as P


def swap(value, axis):
    return lax.ppermute(value, axis, [(0, 1), (1, 0)])


def nt(x, y):
    return lax.dot_general(
        x, y, (((1,), (1,)), ((), ())), preferred_element_type=jnp.float32
    )


def on_device(left_part, vertex, bubble, cross_map):
    momenta = lax.axis_size("mom")
    col = lax.axis_index("col")
    same = lax.axis_index("row") == col
    left, vert = left_part[0], vertex[0]
    half = left.shape[1]
    columns = vert.shape[1]
    per_device = columns // momenta

    left_far = swap(left, "col")
    flipped = vert.T
    flipped_far = swap(flipped, "row")
    scale = bubble.reshape(2, half)
    near_scale = lax.dynamic_index_in_dim(scale, col, 0, keepdims=True)
    far_scale = lax.dynamic_index_in_dim(scale, 1 - col, 0, keepdims=True)
    near = (left.astype(jnp.float32) * near_scale).astype(jnp.bfloat16)
    far = (left_far.astype(jnp.float32) * far_scale).astype(jnp.bfloat16)

    first = nt(jnp.where(same, flipped, flipped_far), near)
    first = first + nt(jnp.where(same, flipped_far, flipped), far)
    rounded = first.astype(jnp.bfloat16)
    rounded_far = swap(rounded, "row")
    second = nt(jnp.where(same, rounded, rounded_far), near)
    second = second + nt(jnp.where(same, rounded_far, rounded), far)
    summed = (flipped.astype(jnp.float32) + first + second).astype(jnp.bfloat16)

    summed = summed.reshape(momenta, per_device, -1)
    received = lax.all_to_all(summed, "mom", split_axis=0, concat_axis=0, tiled=True)
    column = jnp.arange(per_device, dtype=jnp.int32)[:, None]
    source = (cross_map * per_device + column).reshape(-1, 1)
    pick = source == jnp.arange(columns, dtype=jnp.int32)[None, :]
    crossed = jnp.dot(
        pick.astype(jnp.bfloat16),
        received.reshape(columns, -1),
        preferred_element_type=jnp.float32,
    )
    return crossed.astype(jnp.bfloat16).reshape(per_device, momenta, -1)


def solution(mesh):
    in_specs = (
        P("mom", "row", "col"),
        P("mom", "row", "col"),
        P("mom", None),
        P(("col", "mom"), None),
    )
    out_specs = P(("col", "mom"), None, "row")
    return jax.shard_map(
        on_device, mesh=mesh, in_specs=in_specs, out_specs=out_specs, check_vma=False
    )
```

```python
import jax
import jax.numpy as jnp
from jax import lax
from jax.experimental import pallas as pl
from jax.experimental.pallas import tpu as pltpu
from jax.sharding import PartitionSpec as P


LIMIT = pltpu.CompilerParams(vmem_limit_bytes=16 << 20)
VMEM = pl.BlockSpec(memory_space=pltpu.VMEM)
HBM = pl.BlockSpec(memory_space=pltpu.HBM)
ANY = pl.BlockSpec(memory_space=pl.ANY)
BF, F32 = jnp.bfloat16, jnp.float32


def swap(value, axis):
    return lax.ppermute(value, axis, [(0, 1), (1, 0)])


def nt(x, y):
    return lax.dot_general(
        x, y, (((1,), (1,)), ((), ())), preferred_element_type=F32
    )


def local(body, outs, *arrays, aliases=None, flops=0, scratch=()):
    arrays = [pltpu.with_memory_space_constraint(a, pltpu.VMEM) for a in arrays]
    many = isinstance(outs, list)
    return pl.pallas_call(
        body,
        out_shape=outs,
        in_specs=[VMEM] * len(arrays),
        out_specs=[VMEM] * len(outs) if many else VMEM,
        scratch_shapes=scratch,
        input_output_aliases=aliases or {},
        compiler_params=LIMIT,
        cost_estimate=pl.CostEstimate(
            flops=flops, bytes_accessed=1 << 20, transcendentals=0
        ),
    )(*arrays)


def fetch(array, spans):
    def body(source, *refs):
        outs, sem = refs[:-1], refs[-1]
        copies = [
            pltpu.make_async_copy(source.at[s:e, :], out, sem.at[i])
            for i, (out, (s, e)) in enumerate(zip(outs, spans))
        ]
        for copy in copies:
            copy.start()
        for copy in copies:
            copy.wait()

    return pl.pallas_call(
        body,
        out_shape=[
            pltpu.VMEM((e - s, array.shape[1]), array.dtype) for s, e in spans
        ],
        in_specs=[HBM],
        out_specs=[VMEM] * len(spans),
        scratch_shapes=[pltpu.SemaphoreType.DMA((len(spans),))],
        compiler_params=LIMIT,
    )(pltpu.with_memory_space_constraint(array, pltpu.HBM))


def flip_body(vert, out):
    out[...] = vert[...].T


def near_body(left, bubble, flipped, flipped_far, halves, first, other):
    row, col = lax.axis_index("row"), lax.axis_index("col")
    half = left.shape[1]
    scale = bubble[:, pl.ds(pl.multiple_of(col * half, half), half)]
    near = (left[...].astype(F32) * scale).astype(BF)
    halves[col] = near

    @pl.when(row == col)
    def _():
        first[...] = nt(flipped[...], near)
        other[...] = flipped_far[...]

    @pl.when(row != col)
    def _():
        first[...] = nt(flipped_far[...], near)
        other[...] = flipped[...]


def chunk_body(start, stop):
    def body(far, bubble, other, _, __, halves, first, rounded):
        col = 1 - lax.axis_index("col")
        half = far.shape[1]
        scale = bubble[:, pl.ds(pl.multiple_of(col * half, half), half)]
        scaled = (far[...].astype(F32) * scale).astype(BF)
        halves[col, start:stop, :] = scaled
        total = first[:, start:stop] + nt(other[...], scaled)
        first[:, start:stop] = total
        rounded[...] = total.astype(BF)

    return body


def early_body(cuts):
    def body(halves, own0, own1, far0, far1, out):
        row = lax.axis_index("row")
        a, b, _ = cuts
        total = nt(own0[...], halves[row, :b, :a])
        total += nt(far0[...], halves[1 - row, :b, :a])
        total += nt(own1[...], halves[row, :b, a:b])
        total += nt(far1[...], halves[1 - row, :b, a:b])
        out[...] = total

    return body


def late_body(cuts):
    def body(halves, own0, own1, own2, far0, far1, early, flipped, first, out):
        row = lax.axis_index("row")
        a, b, c = cuts
        out[:, :b] = (
            early[...]
            + nt(own2[...], halves[row, :b, b:c])
            + (flipped[:, :b].astype(F32) + first[:, :b])
        )
        total = flipped[:, b:].astype(F32) + first[:, b:]
        total += nt(own0[...], halves[row, b:, :a])
        total += nt(own1[...], halves[row, b:, a:b])
        total += nt(own2[...], halves[row, b:, b:c])
        total += nt(far0[...], halves[1 - row, b:, :a])
        total += nt(far1[...], halves[1 - row, b:, a:b])
        out[:, b:] = total

    return body


def last_body(cuts, partners):
    def body(halves, far2, late, *refs):
        row, mom = lax.axis_index("row"), lax.axis_index("mom")
        _, b, c = cuts
        outs, done = refs[:-1], refs[-1]
        done[...] = (
            late[...] + nt(far2[...], halves[1 - row, :, b:c])
        ).astype(BF)
        size = outs[0].shape[0]
        for out, partner in zip(outs, partners):
            begin = (mom ^ partner) * size if len(outs) > 1 else 0
            out[...] = done[pl.ds(pl.multiple_of(begin, size), size), :]

    return body


def cross_body(partners, momenta, group):
    def body(pick, *refs):
        blocks, (out, gathered, result, sem) = refs[:-4], refs[-4:]
        mom = lax.axis_index("mom")
        per = blocks[0].shape[0]
        copies = []
        for i in range(per // group):
            for block, partner in zip(blocks, partners):
                begin = pl.multiple_of((mom ^ partner) * group, group)
                gathered[i, pl.ds(begin, group), :] = block[
                    i * group : (i + 1) * group, :
                ]
            size = group * momenta
            span = slice(i * size, (i + 1) * size)
            result[span, :] = jnp.dot(
                pick[span, :], gathered[i], preferred_element_type=F32
            ).astype(BF)
            copy = pltpu.make_async_copy(
                result.at[span, :], out.at[span, :], sem.at[i]
            )
            copy.start()
            copies.append(copy)
        for copy in copies:
            copy.wait()

    return body


def xor_partners(momenta):
    def key(k):
        return (-k.bit_length(), int(format(k, "b")[::-1], 2))

    return [0] + sorted(range(1, momenta), key=key)


def pick_body(group):
    def body(cross_map, out):
        momenta, per = cross_map.shape
        wide = (momenta * per, per)
        line = lax.broadcasted_iota(jnp.int32, wide, 0) // momenta
        spread = (line == lax.broadcasted_iota(jnp.int32, wide, 1)).astype(BF)
        known = nt(spread, cross_map[...].astype(F32).astype(BF))
        tall = (momenta * per, momenta)
        line = lax.broadcasted_iota(jnp.int32, tall, 0)
        mine = line % momenta == lax.broadcasted_iota(jnp.int32, tall, 1)
        wanted = jnp.sum(jnp.where(mine, known, 0.0), axis=1, keepdims=True)
        column = (line[:, :1] // momenta) % group
        wanted = wanted.astype(jnp.int32) * group + column
        spot = lax.broadcasted_iota(jnp.int32, out.shape, 1)
        out[...] = jnp.where(spot == wanted, 1.0, 0.0).astype(BF)

    return body


def on_device(left_part, vertex, bubble, cross_map):
    momenta = lax.axis_size("mom")
    left, vert = left_part[0], vertex[0]
    rows, half = left.shape
    columns = vert.shape[1]
    per_device = columns // momenta
    cuts = (rows // 2, rows // 2 + rows // 3, rows)
    square = 2 * columns * half
    starts = (0,) + cuts[:-1]
    spans = list(zip(starts, cuts))

    pieces = fetch(left, spans[:1])
    pieces += fetch(left, spans[1:])
    fars = []
    for piece in pieces:
        fars.append(swap(piece, "col"))
    flipped = local(flip_body, pltpu.VMEM((columns, rows), BF), vert)
    flipped_far = swap(flipped, "row")
    halves, first, other = local(
        near_body,
        [
            pltpu.VMEM((2, rows, half), BF),
            pltpu.VMEM((columns, rows), F32),
            pltpu.VMEM((columns, half), BF),
        ],
        left,
        bubble,
        flipped,
        flipped_far,
        flops=square * rows,
    )
    direct = per_device % 16 == 0 and momenta & (momenta - 1) == 0
    group = 16 * (2 - per_device // 16 % 2) if direct else per_device
    pick = local(
        pick_body(group),
        pltpu.VMEM((columns, momenta * group), BF),
        cross_map.T,
    )
    own, others = [], []

    def arrive(i, halves, first):
        s, e = spans[i]
        halves, first, rounded = local(
            chunk_body(s, e),
            [
                pltpu.VMEM((2, rows, half), BF),
                pltpu.VMEM((columns, rows), F32),
                pltpu.VMEM((columns, e - s), BF),
            ],
            fars[i],
            bubble,
            other,
            halves,
            first,
            aliases={3: 0, 4: 1},
            flops=square * (e - s),
        )
        own.append(rounded)
        others.append(swap(rounded, "row"))
        return halves, first

    halves, first = arrive(0, halves, first)
    halves, first = arrive(1, halves, first)
    early = local(
        early_body(cuts),
        pltpu.VMEM((columns, cuts[1]), F32),
        halves,
        *own,
        *others,
        flops=square * 2 * cuts[1],
    )
    halves, first = arrive(2, halves, first)
    late = local(
        late_body(cuts),
        pltpu.VMEM((columns, rows), F32),
        halves,
        *own,
        *others[:2],
        early,
        flipped,
        first,
        flops=square * (rows - cuts[1]) * 3,
    )
    partners = xor_partners(momenta) if direct else [0]
    size = per_device if direct else columns
    sent = local(
        last_body(cuts, partners),
        [pltpu.VMEM((size, rows), BF)] * len(partners),
        halves,
        others[2],
        late,
        scratch=[pltpu.VMEM((columns, rows), BF)],
    )
    if not direct:
        received = lax.all_to_all(
            sent[0].reshape(momenta, per_device, rows),
            "mom",
            split_axis=0,
            concat_axis=0,
            tiled=True,
        )
        crossed = jnp.dot(
            pick, received.reshape(columns, rows), preferred_element_type=F32
        )
        return crossed.astype(BF).reshape(per_device, momenta, rows)

    got = [sent[0]]
    for block, k in zip(sent[1:], partners[1:]):
        pairs = [(i, i ^ k) for i in range(momenta)]
        got.append(lax.ppermute(block, "mom", pairs))
    crossed = pl.pallas_call(
        cross_body(partners, momenta, group),
        out_shape=jax.ShapeDtypeStruct((columns, rows), BF),
        in_specs=[VMEM] * (1 + momenta),
        out_specs=ANY,
        scratch_shapes=[
            pltpu.VMEM((per_device // group, momenta * group, rows), BF),
            pltpu.VMEM((columns, rows), BF),
            pltpu.SemaphoreType.DMA((per_device // group,)),
        ],
        compiler_params=LIMIT,
    )(*[pltpu.with_memory_space_constraint(a, pltpu.VMEM) for a in (pick, *got)])
    return crossed.reshape(per_device, momenta, rows)


def solution(mesh):
    in_specs = (
        P("mom", "row", "col"),
        P("mom", "row", "col"),
        P("mom", None),
        P(("col", "mom"), None),
    )
    out_specs = P(("col", "mom"), None, "row")
    return jax.shard_map(
        on_device, mesh=mesh, in_specs=in_specs, out_specs=out_specs, check_vma=False
    )
```

```python
import jax
import jax.numpy as jnp
from jax import lax
from jax.experimental import pallas as pl
from jax.experimental.pallas import tpu as pltpu
from jax.sharding import PartitionSpec as P


LIMIT = pltpu.CompilerParams(vmem_limit_bytes=16 << 20)
VMEM = pl.BlockSpec(memory_space=pltpu.VMEM)
HBM = pl.BlockSpec(memory_space=pltpu.HBM)
ANY = pl.BlockSpec(memory_space=pl.ANY)
BF, F32 = jnp.bfloat16, jnp.float32


def swap(value, axis):
    return lax.ppermute(value, axis, [(0, 1), (1, 0)])


def nt(x, y):
    return lax.dot_general(
        x, y, (((1,), (1,)), ((), ())), preferred_element_type=F32
    )


def local(body, outs, *arrays, aliases=None, flops=0, scratch=()):
    arrays = [pltpu.with_memory_space_constraint(a, pltpu.VMEM) for a in arrays]
    many = isinstance(outs, list)
    return pl.pallas_call(
        body,
        out_shape=outs,
        in_specs=[VMEM] * len(arrays),
        out_specs=[VMEM] * len(outs) if many else VMEM,
        scratch_shapes=scratch,
        input_output_aliases=aliases or {},
        compiler_params=LIMIT,
        cost_estimate=pl.CostEstimate(
            flops=flops, bytes_accessed=1 << 20, transcendentals=0
        ),
    )(*arrays)


def fetch(array, spans):
    def body(source, *refs):
        outs, sem = refs[:-1], refs[-1]
        copies = [
            pltpu.make_async_copy(source.at[s:e, :], out, sem.at[i])
            for i, (out, (s, e)) in enumerate(zip(outs, spans))
        ]
        for copy in copies:
            copy.start()
        for copy in copies:
            copy.wait()

    return pl.pallas_call(
        body,
        out_shape=[pltpu.VMEM((e - s, array.shape[1]), array.dtype) for s, e in spans],
        in_specs=[HBM],
        out_specs=[VMEM] * len(spans),
        scratch_shapes=[pltpu.SemaphoreType.DMA((len(spans),))],
        compiler_params=LIMIT,
    )(pltpu.with_memory_space_constraint(array, pltpu.HBM))


def flip_body(vert, out):
    out[...] = vert[...].T


def near_body(left, bubble, flipped, flipped_far, halves, first, other):
    row, col = lax.axis_index("row"), lax.axis_index("col")
    half = left.shape[1]
    scale = bubble[:, pl.ds(pl.multiple_of(col * half, half), half)]
    near = (left[...].astype(F32) * scale).astype(BF)
    halves[col] = near

    @pl.when(row == col)
    def _():
        first[...] = nt(flipped[...], near)
        other[...] = flipped_far[...]

    @pl.when(row != col)
    def _():
        first[...] = nt(flipped_far[...], near)
        other[...] = flipped[...]


def team(mom):
    return ((mom >> 1) ^ (mom >> 2)) & 1


def gated(turn, body):
    def run(*refs):
        @pl.when(team(lax.axis_index("mom")) == turn)
        def _():
            body(*refs)

    return body if turn is None else run


def chunk_body(start, stop, count):
    def body(*refs):
        fars, (bubble, other, _, __, halves, first, rounded) = (
            refs[:count],
            refs[count:],
        )
        col = 1 - lax.axis_index("col")
        half = fars[0].shape[1]
        scale = bubble[:, pl.ds(pl.multiple_of(col * half, half), half)]
        begin = start
        for far in fars:
            end = begin + far.shape[0]
            halves[col, begin:end, :] = (far[...].astype(F32) * scale).astype(BF)
            begin = end
        total = first[:, start:stop] + nt(other[...], halves[col, start:stop, :])
        first[:, start:stop] = total
        rounded[...] = total.astype(BF)

    return body


def early_body(cuts):
    def body(halves, own0, own1, far0, far1, out):
        row = lax.axis_index("row")
        a, b, _ = cuts
        total = nt(own0[...], halves[row, :b, :a])
        total += nt(far0[...], halves[1 - row, :b, :a])
        total += nt(own1[...], halves[row, :b, a:b])
        total += nt(far1[...], halves[1 - row, :b, a:b])
        out[...] = total

    return body


def late_body(cuts):
    def body(halves, own0, own1, own2, far0, far1, early, flipped, first, out):
        row = lax.axis_index("row")
        a, b, c = cuts
        out[:, :b] = (
            early[...]
            + nt(own2[...], halves[row, :b, b:c])
            + (flipped[:, :b].astype(F32) + first[:, :b])
        )
        total = flipped[:, b:].astype(F32) + first[:, b:]
        total += nt(own0[...], halves[row, b:, :a])
        total += nt(own1[...], halves[row, b:, a:b])
        total += nt(own2[...], halves[row, b:, b:c])
        total += nt(far0[...], halves[1 - row, b:, :a])
        total += nt(far1[...], halves[1 - row, b:, a:b])
        out[:, b:] = total

    return body


def last_body(cuts, partners):
    def body(halves, far2, late, *refs):
        row, mom = lax.axis_index("row"), lax.axis_index("mom")
        _, b, c = cuts
        outs, done = refs[:-1], refs[-1]
        done[...] = (
            late[...] + nt(far2[...], halves[1 - row, :, b:c])
        ).astype(BF)
        size = outs[0].shape[0]
        for out, partner in zip(outs, partners):
            begin = pl.multiple_of((mom ^ partner) * size, size)
            out[...] = done[pl.ds(begin, size), :]

    return body


def cross_body(partners, group):
    momenta = len(partners)

    def body(pick, *refs):
        turns = refs[:momenta], refs[momenta : 2 * momenta]
        out, gathered, result, sem = refs[2 * momenta :]
        mom = lax.axis_index("mom")
        groups = out.shape[0] // (momenta * group)
        for turn, blocks in enumerate(turns):
            for block, partner in zip(blocks, partners):
                begin = pl.multiple_of((mom ^ partner) * group, group)

                @pl.when(team(mom ^ partner) == turn)
                def _():
                    for i in range(groups):
                        gathered[i, pl.ds(begin, group), :] = block[
                            i * group : (i + 1) * group, :
                        ]

        copies = []
        for i in range(groups):
            size = group * momenta
            span = slice(i * size, (i + 1) * size)
            result[span, :] = jnp.dot(
                pick[span, :], gathered[i], preferred_element_type=F32
            ).astype(BF)
            copy = pltpu.make_async_copy(
                result.at[span, :], out.at[span, :], sem.at[i]
            )
            copy.start()
            copies.append(copy)
        for copy in copies:
            copy.wait()

    return body


def xor_partners(momenta):
    def key(k):
        return (-k.bit_length(), int(format(k, "b")[::-1], 2))

    return [0] + sorted(range(1, momenta), key=key)


def pick_body(group):
    def body(cross_map, out):
        momenta, per = cross_map.shape
        wide = (momenta * per, per)
        line = lax.broadcasted_iota(jnp.int32, wide, 0) // momenta
        spread = (line == lax.broadcasted_iota(jnp.int32, wide, 1)).astype(BF)
        known = nt(spread, cross_map[...].astype(F32).astype(BF))
        tall = (momenta * per, momenta)
        line = lax.broadcasted_iota(jnp.int32, tall, 0)
        mine = line % momenta == lax.broadcasted_iota(jnp.int32, tall, 1)
        wanted = jnp.sum(jnp.where(mine, known, 0.0), axis=1, keepdims=True)
        column = (line[:, :1] // momenta) % group
        wanted = wanted.astype(jnp.int32) * group + column
        spot = lax.broadcasted_iota(jnp.int32, out.shape, 1)
        out[...] = jnp.where(spot == wanted, 1.0, 0.0).astype(BF)

    return body


def plain(left_part, vertex, bubble, cross_map):
    momenta = lax.axis_size("mom")
    col = lax.axis_index("col")
    same = lax.axis_index("row") == col
    left, flipped = left_part[0], vertex[0].T
    half = left.shape[1]
    columns = flipped.shape[0]
    per_device = columns // momenta

    left_far, flipped_far = swap(left, "col"), swap(flipped, "row")
    scale = bubble.reshape(2, half)
    near_scale = lax.dynamic_index_in_dim(scale, col, 0, keepdims=True)
    far_scale = lax.dynamic_index_in_dim(scale, 1 - col, 0, keepdims=True)
    near = (left.astype(F32) * near_scale).astype(BF)
    far = (left_far.astype(F32) * far_scale).astype(BF)
    first = nt(jnp.where(same, flipped, flipped_far), near)
    first = first + nt(jnp.where(same, flipped_far, flipped), far)
    rounded = first.astype(BF)
    rounded_far = swap(rounded, "row")
    second = nt(jnp.where(same, rounded, rounded_far), near)
    second = second + nt(jnp.where(same, rounded_far, rounded), far)
    summed = (flipped.astype(F32) + first + second).astype(BF)

    summed = summed.reshape(momenta, per_device, -1)
    received = lax.all_to_all(summed, "mom", split_axis=0, concat_axis=0, tiled=True)
    column = jnp.arange(per_device, dtype=jnp.int32)[:, None]
    source = (cross_map * per_device + column).reshape(-1, 1)
    pick = source == jnp.arange(columns, dtype=jnp.int32)[None, :]
    crossed = jnp.dot(
        pick.astype(BF), received.reshape(columns, -1), preferred_element_type=F32
    )
    return crossed.astype(BF).reshape(per_device, momenta, -1)


def staggered(left_part, vertex, bubble, cross_map):
    momenta = lax.axis_size("mom")
    left, vert = left_part[0], vertex[0]
    rows, half = left.shape
    columns = vert.shape[1]
    per_device = columns // momenta
    square = 2 * columns * half
    cuts = (rows // 2, rows // 2 + rows // 3, rows)
    spans = list(zip((0,) + cuts[:-1], cuts))
    relay = cuts[0] + rows // 4
    teams = [[m for m in range(momenta) if team(m) == t] for t in (0, 1)]
    everyone = list(range(momenta))

    def send(value, axes, members, place):
        pairs = [
            (m * 2 + i, place(m, i)[0] * 2 + place(m, i)[1])
            for m in members
            for i in range(2)
        ]
        return lax.ppermute(value, ("mom", axes), pairs)

    def across(m, i):
        return m, 1 - i

    head, detour = fetch(left, [spans[0], (cuts[0], relay)])
    short, tail, wide = fetch(left, [(relay, cuts[1]), spans[2], spans[1]])
    head = send(head, "col", everyone, across)
    detour = send(detour, "col", teams[0], lambda m, i: (m ^ 2, 1 - i))
    arrivals = [
        [
            None,
            send(short, "col", teams[0], across),
            send(tail, "col", teams[0], across),
        ],
        [
            None,
            send(wide, "col", teams[1], across),
            send(tail, "col", teams[1], across),
        ],
    ]
    detour = send(detour, "col", teams[1], lambda m, i: (m ^ 2, i))
    arrivals = [
        [None, [detour, arrivals[0][1]], [arrivals[0][2]]],
        [None, [arrivals[1][1]], [arrivals[1][2]]],
    ]

    flipped = local(flip_body, pltpu.VMEM((columns, rows), BF), vert)
    flipped_far = swap(flipped, "row")
    halves, first, other = local(
        near_body,
        [
            pltpu.VMEM((2, rows, half), BF),
            pltpu.VMEM((columns, rows), F32),
            pltpu.VMEM((columns, half), BF),
        ],
        left,
        bubble,
        flipped,
        flipped_far,
        flops=square * rows,
    )
    group = 16 * (2 - per_device // 16 % 2)
    pick = local(
        pick_body(group), pltpu.VMEM((columns, momenta * group), BF), cross_map.T
    )

    def arrive(i, turn, fars, halves, first):
        s, e = spans[i]
        halves, first, rounded = local(
            gated(turn, chunk_body(s, e, len(fars))),
            [
                pltpu.VMEM((2, rows, half), BF),
                pltpu.VMEM((columns, rows), F32),
                pltpu.VMEM((columns, e - s), BF),
            ],
            *fars,
            bubble,
            other,
            halves,
            first,
            aliases={len(fars) + 2: 0, len(fars) + 3: 1},
            flops=square * (e - s),
        )
        members = everyone if turn is None else teams[turn]
        return halves, first, rounded, send(rounded, "row", members, across)

    halves, first, own0, far0 = arrive(0, None, [head], halves, first)
    partners = xor_partners(momenta)
    received = []
    for turn in (0, 1):
        own, others = [own0], [far0]
        for i in (1, 2):
            halves, first, mine, theirs = arrive(
                i, turn, arrivals[turn][i], halves, first
            )
            own.append(mine)
            others.append(theirs)
            if i == 1:
                early = local(
                    gated(turn, early_body(cuts)),
                    pltpu.VMEM((columns, cuts[1]), F32),
                    halves,
                    *own,
                    *others,
                    flops=square * 2 * cuts[1],
                )
        late = local(
            gated(turn, late_body(cuts)),
            pltpu.VMEM((columns, rows), F32),
            halves,
            *own,
            *others[:2],
            early,
            flipped,
            first,
            flops=square * (rows - cuts[1]) * 3,
        )
        sent = local(
            gated(turn, last_body(cuts, partners)),
            [pltpu.VMEM((per_device, rows), BF)] * momenta,
            halves,
            others[2],
            late,
            scratch=[pltpu.VMEM((columns, rows), BF)],
        )
        received.append(sent[0])
        for block, k in zip(sent[1:], partners[1:]):
            pairs = [(m, m ^ k) for m in teams[turn]]
            received.append(lax.ppermute(block, "mom", pairs))
    arrays = [pick, *received]
    crossed = pl.pallas_call(
        cross_body(partners, group),
        out_shape=jax.ShapeDtypeStruct((columns, rows), BF),
        in_specs=[VMEM] * len(arrays),
        out_specs=ANY,
        scratch_shapes=[
            pltpu.VMEM((per_device // group, momenta * group, rows), BF),
            pltpu.VMEM((columns, rows), BF),
            pltpu.SemaphoreType.DMA((per_device // group,)),
        ],
        compiler_params=LIMIT,
    )(*[pltpu.with_memory_space_constraint(a, pltpu.VMEM) for a in arrays])
    return crossed.reshape(per_device, momenta, rows)


def solution(mesh):
    in_specs = (
        P("mom", "row", "col"),
        P("mom", "row", "col"),
        P("mom", None),
        P(("col", "mom"), None),
    )
    out_specs = P(("col", "mom"), None, "row")

    def step(body):
        return jax.shard_map(
            body, mesh=mesh, in_specs=in_specs, out_specs=out_specs, check_vma=False
        )

    momenta = mesh.shape["mom"]

    def run(left_part, *rest):
        per_device = left_part.shape[1] // momenta
        if per_device % 16 or momenta & (momenta - 1) or momenta < 4:
            return step(plain)(left_part, *rest)
        return step(staggered)(left_part, *rest)

    return run
```

```python
import jax
import jax.numpy as jnp
from jax import lax
from jax.experimental import pallas as pl
from jax.experimental.pallas import tpu as pltpu
from jax.sharding import PartitionSpec as P


LIMIT = pltpu.CompilerParams(vmem_limit_bytes=16 << 20)
VMEM = pl.BlockSpec(memory_space=pltpu.VMEM)
HBM = pl.BlockSpec(memory_space=pltpu.HBM)
ANY = pl.BlockSpec(memory_space=pl.ANY)
BF, F32 = jnp.bfloat16, jnp.float32


def swap(value, axis):
    return lax.ppermute(value, axis, [(0, 1), (1, 0)])


def nt(x, y):
    return lax.dot_general(
        x, y, (((1,), (1,)), ((), ())), preferred_element_type=F32
    )


def local(body, outs, *arrays, aliases=None, flops=0, scratch=()):
    arrays = [pltpu.with_memory_space_constraint(a, pltpu.VMEM) for a in arrays]
    many = isinstance(outs, list)
    return pl.pallas_call(
        body,
        out_shape=outs,
        in_specs=[VMEM] * len(arrays),
        out_specs=[VMEM] * len(outs) if many else VMEM,
        scratch_shapes=scratch,
        input_output_aliases=aliases or {},
        compiler_params=LIMIT,
        cost_estimate=pl.CostEstimate(
            flops=flops, bytes_accessed=1 << 20, transcendentals=0
        ),
    )(*arrays)


def fetch(array, spans):
    def body(source, *refs):
        outs, sem = refs[:-1], refs[-1]
        copies = [
            pltpu.make_async_copy(source.at[s:e, :], out, sem.at[i])
            for i, (out, (s, e)) in enumerate(zip(outs, spans))
        ]
        for copy in copies:
            copy.start()
        for copy in copies:
            copy.wait()

    return pl.pallas_call(
        body,
        out_shape=[pltpu.VMEM((e - s, array.shape[1]), array.dtype) for s, e in spans],
        in_specs=[HBM],
        out_specs=[VMEM] * len(spans),
        scratch_shapes=[pltpu.SemaphoreType.DMA((len(spans),))],
        compiler_params=LIMIT,
    )(pltpu.with_memory_space_constraint(array, pltpu.HBM))


def flip_body(vert, out):
    out[...] = vert[...].T


def near_body(left, bubble, flipped, flipped_far, halves, first, other):
    row, col = lax.axis_index("row"), lax.axis_index("col")
    half = left.shape[1]
    scale = bubble[:, pl.ds(pl.multiple_of(col * half, half), half)]
    near = (left[...].astype(F32) * scale).astype(BF)
    halves[col] = near

    @pl.when(row == col)
    def _():
        first[...] = nt(flipped[...], near)
        other[...] = flipped_far[...]

    @pl.when(row != col)
    def _():
        first[...] = nt(flipped_far[...], near)
        other[...] = flipped[...]


def chunk_body(start, stop):
    def body(far, bubble, other, _, __, halves, first, rounded):
        col = 1 - lax.axis_index("col")
        half = far.shape[1]
        scale = bubble[:, pl.ds(pl.multiple_of(col * half, half), half)]
        scaled = (far[...].astype(F32) * scale).astype(BF)
        halves[col, start:stop, :] = scaled
        total = first[:, start:stop] + nt(other[...], scaled)
        first[:, start:stop] = total
        rounded[...] = total.astype(BF)

    return body


def add_body(spans, i, final):
    def body(*refs):
        row = lax.axis_index("row")
        count = i + 1
        own, refs = refs[:count], refs[count:]
        far, refs = refs[: count - final], refs[count - final :]
        halves, flipped, first, total = refs[0], refs[1], refs[2], refs[-1]
        start, stop = spans[i]
        for s, e in [(0, start)] if start else []:
            part = total[:, s:e] + nt(own[i][...], halves[row, s:e, start:stop])
            if not final:
                part += nt(far[i][...], halves[1 - row, s:e, start:stop])
            total[:, s:e] = part
        part = flipped[:, start:stop].astype(F32) + first[:, start:stop]
        for half, terms in ((row, own), (1 - row, far)):
            for term, (s, e) in zip(terms, spans):
                part += nt(term[...], halves[half, start:stop, s:e])
        total[:, start:stop] = part

    return body


def last_body(span, partners):
    def body(halves, far, total, *outs):
        row, mom = lax.axis_index("row"), lax.axis_index("mom")
        s, e = span
        size = outs[0].shape[0]
        weights = halves[1 - row, :, s:e]
        for out, partner in zip(outs, partners):
            begin = pl.multiple_of((mom ^ partner) * size, size)
            lines = pl.ds(begin, size)
            out[...] = (total[lines, :] + nt(far[lines, :], weights)).astype(BF)

    return body


def cross_body(partners, group):
    momenta = len(partners)

    def body(pick, *refs):
        blocks, (out, gathered, result, sem) = refs[:momenta], refs[momenta:]
        mom = lax.axis_index("mom")
        groups = out.shape[0] // (momenta * group)
        size = group * momenta
        copies = []
        for i in range(groups):
            for block, partner in zip(blocks, partners):
                begin = pl.multiple_of((mom ^ partner) * group, group)
                gathered[i, pl.ds(begin, group), :] = block[
                    i * group : (i + 1) * group, :
                ]
            span = slice(i * size, (i + 1) * size)
            result[span, :] = jnp.dot(
                pick[span, :], gathered[i], preferred_element_type=F32
            ).astype(BF)
            copy = pltpu.make_async_copy(
                result.at[span, :], out.at[span, :], sem.at[i]
            )
            copy.start()
            copies.append(copy)
        for copy in copies:
            copy.wait()

    return body


def xor_partners(momenta):
    def key(k):
        return (-k.bit_length(), int(format(k, "b")[::-1], 2))

    return [0] + sorted(range(1, momenta), key=key)


def pick_body(group):
    def body(cross_map, out):
        momenta, per = cross_map.shape
        wide = (momenta * per, per)
        line = lax.broadcasted_iota(jnp.int32, wide, 0) // momenta
        spread = (line == lax.broadcasted_iota(jnp.int32, wide, 1)).astype(BF)
        known = nt(spread, cross_map[...].astype(F32).astype(BF))
        tall = (momenta * per, momenta)
        line = lax.broadcasted_iota(jnp.int32, tall, 0)
        mine = line % momenta == lax.broadcasted_iota(jnp.int32, tall, 1)
        wanted = jnp.sum(jnp.where(mine, known, 0.0), axis=1, keepdims=True)
        column = (line[:, :1] // momenta) % group
        wanted = wanted.astype(jnp.int32) * group + column
        spot = lax.broadcasted_iota(jnp.int32, out.shape, 1)
        out[...] = jnp.where(spot == wanted, 1.0, 0.0).astype(BF)

    return body


def plain(left_part, vertex, bubble, cross_map):
    momenta = lax.axis_size("mom")
    col = lax.axis_index("col")
    same = lax.axis_index("row") == col
    left, flipped = left_part[0], vertex[0].T
    half = left.shape[1]
    columns = flipped.shape[0]
    per_device = columns // momenta

    left_far, flipped_far = swap(left, "col"), swap(flipped, "row")
    scale = bubble.reshape(2, half)
    near_scale = lax.dynamic_index_in_dim(scale, col, 0, keepdims=True)
    far_scale = lax.dynamic_index_in_dim(scale, 1 - col, 0, keepdims=True)
    near = (left.astype(F32) * near_scale).astype(BF)
    far = (left_far.astype(F32) * far_scale).astype(BF)
    first = nt(jnp.where(same, flipped, flipped_far), near)
    first = first + nt(jnp.where(same, flipped_far, flipped), far)
    rounded = first.astype(BF)
    rounded_far = swap(rounded, "row")
    second = nt(jnp.where(same, rounded, rounded_far), near)
    second = second + nt(jnp.where(same, rounded_far, rounded), far)
    summed = (flipped.astype(F32) + first + second).astype(BF)

    summed = summed.reshape(momenta, per_device, -1)
    received = lax.all_to_all(summed, "mom", split_axis=0, concat_axis=0, tiled=True)
    column = jnp.arange(per_device, dtype=jnp.int32)[:, None]
    source = (cross_map * per_device + column).reshape(-1, 1)
    pick = source == jnp.arange(columns, dtype=jnp.int32)[None, :]
    crossed = jnp.dot(
        pick.astype(BF), received.reshape(columns, -1), preferred_element_type=F32
    )
    return crossed.astype(BF).reshape(per_device, momenta, -1)


def tiled(left_part, vertex, bubble, cross_map):
    momenta = lax.axis_size("mom")
    left, vert = left_part[0], vertex[0]
    rows, half = left.shape
    columns = vert.shape[1]
    per_device = columns // momenta
    square = 2 * columns * half
    unit = rows // 6
    cuts = (0, unit, 3 * unit, 5 * unit, rows)
    spans = list(zip(cuts, cuts[1:]))

    pieces = fetch(left, spans[:1])
    pieces += fetch(left, spans[1:])
    fars = []
    for piece in pieces:
        fars.append(swap(piece, "col"))
    flipped = local(flip_body, pltpu.VMEM((columns, rows), BF), vert)
    flipped_far = swap(flipped, "row")
    halves, first, other = local(
        near_body,
        [
            pltpu.VMEM((2, rows, half), BF),
            pltpu.VMEM((columns, rows), F32),
            pltpu.VMEM((columns, half), BF),
        ],
        left,
        bubble,
        flipped,
        flipped_far,
        flops=square * rows,
    )
    group = 16 * (2 - per_device // 16 % 2)
    pick = local(
        pick_body(group), pltpu.VMEM((columns, momenta * group), BF), cross_map.T
    )
    own, others, total = [], [], None
    for i, (s, e) in enumerate(spans):
        halves, first, rounded = local(
            chunk_body(s, e),
            [
                pltpu.VMEM((2, rows, half), BF),
                pltpu.VMEM((columns, rows), F32),
                pltpu.VMEM((columns, e - s), BF),
            ],
            fars[i],
            bubble,
            other,
            halves,
            first,
            aliases={3: 0, 4: 1},
            flops=square * (e - s),
        )
        own.append(rounded)
        others.append(swap(rounded, "row"))
        final = e == rows
        inputs = [*own, *others[: len(own) - final], halves, flipped, first]
        total = local(
            add_body(spans, i, final),
            pltpu.VMEM((columns, rows), F32),
            *inputs,
            *([] if total is None else [total]),
            aliases={} if total is None else {len(inputs): 0},
            flops=square * 2 * (e - s),
        )

    partners = xor_partners(momenta)
    order = partners[1:] + partners[:1]
    sent = []
    for chosen in (order[:1], order[1:]):
        sent += local(
            last_body(spans[-1], chosen),
            [pltpu.VMEM((per_device, rows), BF)] * len(chosen),
            halves,
            others[-1],
            total,
            flops=square * unit * len(chosen) // momenta,
        )
    got = []
    for block, k in zip(sent, order[:-1]):
        pairs = [(i, i ^ k) for i in range(momenta)]
        got.append(lax.ppermute(block, "mom", pairs))
    arrays = [pick, *got, sent[-1]]
    crossed = pl.pallas_call(
        cross_body(order, group),
        out_shape=jax.ShapeDtypeStruct((columns, rows), BF),
        in_specs=[VMEM] * len(arrays),
        out_specs=ANY,
        scratch_shapes=[
            pltpu.VMEM((per_device // group, momenta * group, rows), BF),
            pltpu.VMEM((columns, rows), BF),
            pltpu.SemaphoreType.DMA((per_device // group,)),
        ],
        compiler_params=LIMIT,
    )(*[pltpu.with_memory_space_constraint(a, pltpu.VMEM) for a in arrays])
    return crossed.reshape(per_device, momenta, rows)


def solution(mesh):
    in_specs = (
        P("mom", "row", "col"),
        P("mom", "row", "col"),
        P("mom", None),
        P(("col", "mom"), None),
    )
    out_specs = P(("col", "mom"), None, "row")

    def step(body):
        return jax.shard_map(
            body, mesh=mesh, in_specs=in_specs, out_specs=out_specs, check_vma=False
        )

    momenta = mesh.shape["mom"]

    def run(left_part, *rest):
        per_device = left_part.shape[1] // momenta
        if per_device % 16 or momenta & (momenta - 1) or momenta < 2:
            return step(plain)(left_part, *rest)
        return step(tiled)(left_part, *rest)

    return run
```

```python
import jax
import jax.numpy as jnp
from jax import lax
from jax.experimental import pallas as pl
from jax.experimental.pallas import tpu as pltpu
from jax.sharding import PartitionSpec as P


LIMIT = pltpu.CompilerParams(vmem_limit_bytes=16 << 20)
VMEM = pl.BlockSpec(memory_space=pltpu.VMEM)
HBM = pl.BlockSpec(memory_space=pltpu.HBM)
ANY = pl.BlockSpec(memory_space=pl.ANY)
BF, F32 = jnp.bfloat16, jnp.float32


def swap(value, axis):
    return lax.ppermute(value, axis, [(0, 1), (1, 0)])


def nt(x, y):
    return lax.dot_general(
        x, y, (((1,), (1,)), ((), ())), preferred_element_type=F32
    )


def local(body, outs, *arrays, aliases=None, flops=0, scratch=()):
    arrays = [pltpu.with_memory_space_constraint(a, pltpu.VMEM) for a in arrays]
    many = isinstance(outs, list)
    return pl.pallas_call(
        body,
        out_shape=outs,
        in_specs=[VMEM] * len(arrays),
        out_specs=[VMEM] * len(outs) if many else VMEM,
        scratch_shapes=scratch,
        input_output_aliases=aliases or {},
        compiler_params=LIMIT,
        cost_estimate=pl.CostEstimate(
            flops=flops, bytes_accessed=1 << 20, transcendentals=0
        ),
    )(*arrays)


def fetch(array, spans):
    def body(source, *refs):
        outs, sem = refs[:-1], refs[-1]
        copies = [
            pltpu.make_async_copy(source.at[s:e, :], out, sem.at[i])
            for i, (out, (s, e)) in enumerate(zip(outs, spans))
        ]
        for copy in copies:
            copy.start()
        for copy in copies:
            copy.wait()

    return pl.pallas_call(
        body,
        out_shape=[pltpu.VMEM((e - s, array.shape[1]), array.dtype) for s, e in spans],
        in_specs=[HBM],
        out_specs=[VMEM] * len(spans),
        scratch_shapes=[pltpu.SemaphoreType.DMA((len(spans),))],
        compiler_params=LIMIT,
    )(pltpu.with_memory_space_constraint(array, pltpu.HBM))


def flip_body(vert, out):
    out[...] = vert[...].T


def near_body(left, bubble, flipped, flipped_far, halves, first, other):
    row, col = lax.axis_index("row"), lax.axis_index("col")
    half = left.shape[1]
    scale = bubble[:, pl.ds(pl.multiple_of(col * half, half), half)]
    near = (left[...].astype(F32) * scale).astype(BF)
    halves[col] = near

    @pl.when(row == col)
    def _():
        first[...] = nt(flipped[...], near)
        other[...] = flipped_far[...]

    @pl.when(row != col)
    def _():
        first[...] = nt(flipped_far[...], near)
        other[...] = flipped[...]


def chunk_body(start, stop):
    def body(far, bubble, other, _, __, halves, first, rounded):
        col = 1 - lax.axis_index("col")
        half = far.shape[1]
        scale = bubble[:, pl.ds(pl.multiple_of(col * half, half), half)]
        scaled = (far[...].astype(F32) * scale).astype(BF)
        halves[col, start:stop, :] = scaled
        total = first[:, start:stop] + nt(other[...], scaled)
        first[:, start:stop] = total
        rounded[...] = total.astype(BF)

    return body


def add_body(spans, i, final):
    def body(*refs):
        row = lax.axis_index("row")
        count = i + 1
        own, refs = refs[:count], refs[count:]
        far, refs = refs[: count - final], refs[count - final :]
        halves, flipped, first, total = refs[0], refs[1], refs[2], refs[-1]
        start, stop = spans[i]
        for s, e in [(0, start)] if start else []:
            part = total[:, s:e] + nt(own[i][...], halves[row, s:e, start:stop])
            if not final:
                part += nt(far[i][...], halves[1 - row, s:e, start:stop])
            total[:, s:e] = part
        part = flipped[:, start:stop].astype(F32) + first[:, start:stop]
        for half, terms in ((row, own), (1 - row, far)):
            for term, (s, e) in zip(terms, spans):
                part += nt(term[...], halves[half, start:stop, s:e])
        total[:, start:stop] = part

    return body


def last_body(span, steps):
    def body(halves, far, total, *outs):
        row, mom = lax.axis_index("row"), lax.axis_index("mom")
        s, e = span
        size = outs[0].shape[0]
        weights = halves[1 - row, :, s:e]
        for out, step in zip(outs, steps):
            begin = pl.multiple_of(meet(mom, step) * size, size)
            lines = pl.ds(begin, size)
            out[...] = (total[lines, :] + nt(far[lines, :], weights)).astype(BF)

    return body


def cross_body(steps, group):
    momenta = len(steps)

    def body(pick, *refs):
        blocks, (out, gathered, result, sem) = refs[:momenta], refs[momenta:]
        mom = lax.axis_index("mom")
        groups = out.shape[0] // (momenta * group)
        size = group * momenta
        copies = []
        for i in range(groups):
            for block, step in zip(blocks, steps):
                begin = pl.multiple_of(meet(mom, step) * group, group)
                gathered[i, pl.ds(begin, group), :] = block[
                    i * group : (i + 1) * group, :
                ]
            span = slice(i * size, (i + 1) * size)
            result[span, :] = jnp.dot(
                pick[span, :], gathered[i], preferred_element_type=F32
            ).astype(BF)
            copy = pltpu.make_async_copy(
                result.at[span, :], out.at[span, :], sem.at[i]
            )
            copy.start()
            copies.append(copy)
        for copy in copies:
            copy.wait()

    return body


def team(mom):
    return ((mom >> 1) ^ (mom >> 2)) & 1


def meet(mom, step):
    outer, inner = step
    return mom ^ (outer + team(mom) * (inner - outer))


def steps_of(momenta):
    def key(k):
        return (-k.bit_length(), int(format(k, "b")[::-1], 2))

    steps = [(k, k) for k in sorted(range(1, momenta), key=key)]
    if momenta >= 8:
        far = momenta - 2
        mixed = [(1, far), (far, 1)]
        steps = [k for k in steps if k[0] not in (1, far)]
        steps = mixed[:1] + [(4, 4), (2, 2), (5, 5)] + mixed[1:] + [(3, 3), (7, 7)]
    return steps


def pick_body(group):
    def body(cross_map, out):
        momenta, per = cross_map.shape
        wide = (momenta * per, per)
        line = lax.broadcasted_iota(jnp.int32, wide, 0) // momenta
        spread = (line == lax.broadcasted_iota(jnp.int32, wide, 1)).astype(BF)
        known = nt(spread, cross_map[...].astype(F32).astype(BF))
        tall = (momenta * per, momenta)
        line = lax.broadcasted_iota(jnp.int32, tall, 0)
        mine = line % momenta == lax.broadcasted_iota(jnp.int32, tall, 1)
        wanted = jnp.sum(jnp.where(mine, known, 0.0), axis=1, keepdims=True)
        column = (line[:, :1] // momenta) % group
        wanted = wanted.astype(jnp.int32) * group + column
        spot = lax.broadcasted_iota(jnp.int32, out.shape, 1)
        out[...] = jnp.where(spot == wanted, 1.0, 0.0).astype(BF)

    return body


def plain(left_part, vertex, bubble, cross_map):
    momenta = lax.axis_size("mom")
    col = lax.axis_index("col")
    same = lax.axis_index("row") == col
    left, flipped = left_part[0], vertex[0].T
    half = left.shape[1]
    columns = flipped.shape[0]
    per_device = columns // momenta

    left_far, flipped_far = swap(left, "col"), swap(flipped, "row")
    scale = bubble.reshape(2, half)
    near_scale = lax.dynamic_index_in_dim(scale, col, 0, keepdims=True)
    far_scale = lax.dynamic_index_in_dim(scale, 1 - col, 0, keepdims=True)
    near = (left.astype(F32) * near_scale).astype(BF)
    far = (left_far.astype(F32) * far_scale).astype(BF)
    first = nt(jnp.where(same, flipped, flipped_far), near)
    first = first + nt(jnp.where(same, flipped_far, flipped), far)
    rounded = first.astype(BF)
    rounded_far = swap(rounded, "row")
    second = nt(jnp.where(same, rounded, rounded_far), near)
    second = second + nt(jnp.where(same, rounded_far, rounded), far)
    summed = (flipped.astype(F32) + first + second).astype(BF)

    summed = summed.reshape(momenta, per_device, -1)
    received = lax.all_to_all(summed, "mom", split_axis=0, concat_axis=0, tiled=True)
    column = jnp.arange(per_device, dtype=jnp.int32)[:, None]
    source = (cross_map * per_device + column).reshape(-1, 1)
    pick = source == jnp.arange(columns, dtype=jnp.int32)[None, :]
    crossed = jnp.dot(
        pick.astype(BF), received.reshape(columns, -1), preferred_element_type=F32
    )
    return crossed.astype(BF).reshape(per_device, momenta, -1)


def tiled(left_part, vertex, bubble, cross_map):
    momenta = lax.axis_size("mom")
    left, vert = left_part[0], vertex[0]
    rows, half = left.shape
    columns = vert.shape[1]
    per_device = columns // momenta
    square = 2 * columns * half
    unit = rows // 6
    cuts = (0, unit, 3 * unit, 4 * unit, 5 * unit, rows)
    spans = list(zip(cuts, cuts[1:]))

    pieces = fetch(left, spans[:1])
    pieces += fetch(left, spans[1:])
    fars = []
    for piece in pieces:
        fars.append(swap(piece, "col"))
    flipped = local(flip_body, pltpu.VMEM((columns, rows), BF), vert)
    flipped_far = swap(flipped, "row")
    halves, first, other = local(
        near_body,
        [
            pltpu.VMEM((2, rows, half), BF),
            pltpu.VMEM((columns, rows), F32),
            pltpu.VMEM((columns, half), BF),
        ],
        left,
        bubble,
        flipped,
        flipped_far,
        flops=square * rows,
    )
    group = 16 * (2 - per_device // 16 % 2)
    pick = local(
        pick_body(group), pltpu.VMEM((columns, momenta * group), BF), cross_map.T
    )
    own, others, total = [], [], None
    for i, (s, e) in enumerate(spans):
        halves, first, rounded = local(
            chunk_body(s, e),
            [
                pltpu.VMEM((2, rows, half), BF),
                pltpu.VMEM((columns, rows), F32),
                pltpu.VMEM((columns, e - s), BF),
            ],
            fars[i],
            bubble,
            other,
            halves,
            first,
            aliases={3: 0, 4: 1},
            flops=square * (e - s),
        )
        own.append(rounded)
        others.append(swap(rounded, "row"))
        final = e == rows
        inputs = [*own, *others[: len(own) - final], halves, flipped, first]
        total = local(
            add_body(spans, i, final),
            pltpu.VMEM((columns, rows), F32),
            *inputs,
            *([] if total is None else [total]),
            aliases={} if total is None else {len(inputs): 0},
            flops=square * 2 * (e - s),
        )

    order = steps_of(momenta) + [(0, 0)]
    sent = []
    for chosen in (order[:1], order[1:]):
        sent += local(
            last_body(spans[-1], chosen),
            [pltpu.VMEM((per_device, rows), BF)] * len(chosen),
            halves,
            others[-1],
            total,
            flops=square * unit * len(chosen) // momenta,
        )
    got = []
    for block, step in zip(sent, order[:-1]):
        pairs = [(m, meet(m, step)) for m in range(momenta)]
        got.append(lax.ppermute(block, "mom", pairs))
    arrays = [pick, *got, sent[-1]]
    crossed = pl.pallas_call(
        cross_body(order, group),
        out_shape=jax.ShapeDtypeStruct((columns, rows), BF),
        in_specs=[VMEM] * len(arrays),
        out_specs=ANY,
        scratch_shapes=[
            pltpu.VMEM((per_device // group, momenta * group, rows), BF),
            pltpu.VMEM((columns, rows), BF),
            pltpu.SemaphoreType.DMA((per_device // group,)),
        ],
        compiler_params=LIMIT,
    )(*[pltpu.with_memory_space_constraint(a, pltpu.VMEM) for a in arrays])
    return crossed.reshape(per_device, momenta, rows)


def solution(mesh):
    in_specs = (
        P("mom", "row", "col"),
        P("mom", "row", "col"),
        P("mom", None),
        P(("col", "mom"), None),
    )
    out_specs = P(("col", "mom"), None, "row")

    def step(body):
        return jax.shard_map(
            body, mesh=mesh, in_specs=in_specs, out_specs=out_specs, check_vma=False
        )

    momenta = mesh.shape["mom"]

    def run(left_part, *rest):
        per_device = left_part.shape[1] // momenta
        if per_device % 16 or momenta & (momenta - 1) or momenta < 2:
            return step(plain)(left_part, *rest)
        return step(tiled)(
            left_part, *rest
        )

    return run
```

```python
import jax
import jax.numpy as jnp
from jax import lax
from jax.experimental import pallas as pl
from jax.experimental.pallas import tpu as pltpu
from jax.sharding import PartitionSpec as P


LIMIT = pltpu.CompilerParams(vmem_limit_bytes=16 << 20)
VMEM = pl.BlockSpec(memory_space=pltpu.VMEM)
HBM = pl.BlockSpec(memory_space=pltpu.HBM)
ANY = pl.BlockSpec(memory_space=pl.ANY)
BF, F32 = jnp.bfloat16, jnp.float32


def swap(value, axis):
    return lax.ppermute(value, axis, [(0, 1), (1, 0)])


def nt(x, y):
    return lax.dot_general(
        x, y, (((1,), (1,)), ((), ())), preferred_element_type=F32
    )


def local(body, outs, *arrays, aliases=None, flops=0, scratch=()):
    arrays = [pltpu.with_memory_space_constraint(a, pltpu.VMEM) for a in arrays]
    many = isinstance(outs, list)
    return pl.pallas_call(
        body,
        out_shape=outs,
        in_specs=[VMEM] * len(arrays),
        out_specs=[VMEM] * len(outs) if many else VMEM,
        scratch_shapes=scratch,
        input_output_aliases=aliases or {},
        compiler_params=LIMIT,
        cost_estimate=pl.CostEstimate(
            flops=flops, bytes_accessed=1 << 20, transcendentals=0
        ),
    )(*arrays)


def fetch(array, spans):
    def body(source, *refs):
        outs, sem = refs[:-1], refs[-1]
        copies = [
            pltpu.make_async_copy(source.at[s:e, :], out, sem.at[i])
            for i, (out, (s, e)) in enumerate(zip(outs, spans))
        ]
        for copy in copies:
            copy.start()
        for copy in copies:
            copy.wait()

    return pl.pallas_call(
        body,
        out_shape=[pltpu.VMEM((e - s, array.shape[1]), array.dtype) for s, e in spans],
        in_specs=[HBM],
        out_specs=[VMEM] * len(spans),
        scratch_shapes=[pltpu.SemaphoreType.DMA((len(spans),))],
        compiler_params=LIMIT,
    )(pltpu.with_memory_space_constraint(array, pltpu.HBM))


def flip_body(vert, out):
    out[...] = vert[...].T


def near_body(left, bubble, flipped, flipped_far, halves, first, other):
    row, col = lax.axis_index("row"), lax.axis_index("col")
    half = left.shape[1]
    scale = bubble[:, pl.ds(pl.multiple_of(col * half, half), half)]
    near = (left[...].astype(F32) * scale).astype(BF)
    halves[col] = near

    @pl.when(row == col)
    def _():
        first[...] = nt(flipped[...], near)
        other[...] = flipped_far[...]

    @pl.when(row != col)
    def _():
        first[...] = nt(flipped_far[...], near)
        other[...] = flipped[...]


def chunk_body(start, stop):
    def body(far, bubble, other, *refs):
        halves, first, rounded = refs[-3:]
        col = 1 - lax.axis_index("col")
        half = far.shape[1]
        scale = bubble[:, pl.ds(pl.multiple_of(col * half, half), half)]
        scaled = (far[...].astype(F32) * scale).astype(BF)
        halves[col, start:stop, :] = scaled
        total = first[:, start:stop] + nt(other[...], scaled)
        first[:, start:stop] = total
        rounded[...] = total.astype(BF)

    return body


def add_body(spans, i):
    def body(*refs):
        row = lax.axis_index("row")
        own, refs = refs[: i + 1], refs[i + 1 :]
        far, refs = refs[:i], refs[i:]
        halves, flipped, first, total = refs[0], refs[1], refs[2], refs[-1]
        start, stop = spans[i]
        if i:
            s, e = spans[i - 1]
            part = total[:, :start] + nt(own[i][...], halves[row, :start, start:stop])
            part += nt(far[i - 1][...], halves[1 - row, :start, s:e])
            total[:, :start] = part
        part = flipped[:, start:stop].astype(F32) + first[:, start:stop]
        for half, terms in ((row, own), (1 - row, far)):
            for term, (s, e) in zip(terms, spans):
                part += nt(term[...], halves[half, start:stop, s:e])
        total[:, start:stop] = part

    return body


def settle_body(span):
    def body(halves, far, _, total):
        other = 1 - lax.axis_index("row")
        s, e = span
        total[:, :e] += nt(far[...], halves[other, :e, s:e])

    return body


def peek_body(step, start):
    def body(far, bubble, other, first, out):
        col, mom = 1 - lax.axis_index("col"), lax.axis_index("mom")
        half, size = far.shape[1], out.shape[0]
        scale = bubble[:, pl.ds(pl.multiple_of(col * half, half), half)]
        scaled = (far[...].astype(F32) * scale).astype(BF)
        lines = pl.ds(pl.multiple_of(meet(mom, step) * size, size), size)
        out[...] = (first[lines, start:] + nt(other[lines, :], scaled)).astype(BF)

    return body


def own_body(spans, step):
    def body(*refs):
        row, mom = lax.axis_index("row"), lax.axis_index("mom")
        count = len(spans)
        own, far, refs = refs[:count], refs[count : 2 * count - 1], refs[2 * count - 1 :]
        halves, flipped, first, total, size_like, out = refs
        start, stop = spans[-1]
        size = size_like.shape[0]
        lines = pl.ds(pl.multiple_of(meet(mom, step) * size, size), size)
        out[:, :start] = total[lines, :start] + nt(
            own[-1][lines, :], halves[row, :start, start:stop]
        )
        part = flipped[lines, start:stop].astype(F32) + first[lines, start:stop]
        for half, terms in ((row, own), (1 - row, far)):
            for term, (s, e) in zip(terms, spans):
                part += nt(term[lines, :], halves[half, start:stop, s:e])
        out[:, start:] = part

    return body


def close_body(span):
    def body(halves, last, part, out):
        s, e = span
        weights = halves[1 - lax.axis_index("row"), :, s:e]
        out[...] = (part[...] + nt(last[...], weights)).astype(BF)

    return body


def finish_body(spans, steps):
    def body(*refs):
        row, mom = lax.axis_index("row"), lax.axis_index("mom")
        count = len(spans)
        own, far, refs = refs[:count], refs[count : 2 * count], refs[2 * count :]
        halves, flipped, first, total = refs[:4]
        outs = refs[4:]
        start, stop = spans[-1]
        size = outs[0].shape[0]
        done = None
        if len(steps) > 2:
            outs, done = outs[:-1], outs[-1]
        blocks = [done] if done is not None else outs
        for out, step in zip(blocks, steps):
            begin = 0 if done is not None else meet(mom, step) * size
            lines = pl.ds(pl.multiple_of(begin, size), out.shape[0])
            part = total[lines, :start]
            part += nt(own[-1][lines, :], halves[row, :start, start:stop])
            part += nt(far[-1][lines, :], halves[1 - row, :start, start:stop])
            out[:, :start] = part.astype(BF)
            part = flipped[lines, start:stop].astype(F32) + first[lines, start:stop]
            for half, terms in ((row, own), (1 - row, far)):
                for term, (s, e) in zip(terms, spans):
                    part += nt(term[lines, :], halves[half, start:stop, s:e])
            out[:, start:] = part.astype(BF)
        if done is not None:
            for out, step in zip(outs, steps):
                begin = pl.multiple_of(meet(mom, step) * size, size)
                out[...] = done[pl.ds(begin, size), :]

    return body


def cross_body(steps, group):
    momenta = len(steps)

    def body(pick, *refs):
        blocks, (out, gathered, result, sem) = refs[:momenta], refs[momenta:]
        mom = lax.axis_index("mom")
        groups = out.shape[0] // (momenta * group)
        size = group * momenta
        copies = []
        for i in range(groups):
            for block, step in zip(blocks, steps):
                begin = pl.multiple_of(meet(mom, step) * group, group)
                gathered[i, pl.ds(begin, group), :] = block[
                    i * group : (i + 1) * group, :
                ]
            span = slice(i * size, (i + 1) * size)
            width = out.shape[1] // 2
            for j in range(2):
                lanes = slice(j * width, (j + 1) * width)
                result[span, lanes] = jnp.dot(
                    pick[span, :], gathered[i, :, lanes], preferred_element_type=F32
                ).astype(BF)
                copy = pltpu.make_async_copy(
                    result.at[span, lanes], out.at[span, lanes], sem.at[2 * i + j]
                )
                copy.start()
                copies.append(copy)
        for copy in copies:
            copy.wait()

    return body


def team(mom):
    return ((mom >> 1) ^ (mom >> 2)) & 1


def meet(mom, step):
    outer, inner = step
    return mom ^ (outer + team(mom) * (inner - outer))


def steps_of(momenta):
    def key(k):
        return (-k.bit_length(), int(format(k, "b")[::-1], 2))

    steps = [(k, k) for k in sorted(range(1, momenta), key=key)]
    if momenta >= 8:
        far = momenta - 2
        mixed = [(1, far), (far, 1)]
        steps = [k for k in steps if k[0] not in (1, far)]
        steps = mixed[:1] + [(4, 4), (2, 2), (5, 5), (3, 3)] + mixed[1:] + [(7, 7)]
    return steps


def pick_body(group):
    def body(cross_map, out):
        momenta, per = cross_map.shape
        wide = (momenta * per, per)
        line = lax.broadcasted_iota(jnp.int32, wide, 0) // momenta
        spread = (line == lax.broadcasted_iota(jnp.int32, wide, 1)).astype(BF)
        known = nt(spread, cross_map[...].astype(F32).astype(BF))
        tall = (momenta * per, momenta)
        line = lax.broadcasted_iota(jnp.int32, tall, 0)
        mine = line % momenta == lax.broadcasted_iota(jnp.int32, tall, 1)
        wanted = jnp.sum(jnp.where(mine, known, 0.0), axis=1, keepdims=True)
        column = (line[:, :1] // momenta) % group
        wanted = wanted.astype(jnp.int32) * group + column
        spot = lax.broadcasted_iota(jnp.int32, out.shape, 1)
        out[...] = jnp.where(spot == wanted, 1.0, 0.0).astype(BF)

    return body


def plain(left_part, vertex, bubble, cross_map):
    momenta = lax.axis_size("mom")
    col = lax.axis_index("col")
    same = lax.axis_index("row") == col
    left, flipped = left_part[0], vertex[0].T
    half = left.shape[1]
    columns = flipped.shape[0]
    per_device = columns // momenta

    left_far, flipped_far = swap(left, "col"), swap(flipped, "row")
    scale = bubble.reshape(2, half)
    near_scale = lax.dynamic_index_in_dim(scale, col, 0, keepdims=True)
    far_scale = lax.dynamic_index_in_dim(scale, 1 - col, 0, keepdims=True)
    near = (left.astype(F32) * near_scale).astype(BF)
    far = (left_far.astype(F32) * far_scale).astype(BF)
    first = nt(jnp.where(same, flipped, flipped_far), near)
    first = first + nt(jnp.where(same, flipped_far, flipped), far)
    rounded = first.astype(BF)
    rounded_far = swap(rounded, "row")
    second = nt(jnp.where(same, rounded, rounded_far), near)
    second = second + nt(jnp.where(same, rounded_far, rounded), far)
    summed = (flipped.astype(F32) + first + second).astype(BF)

    summed = summed.reshape(momenta, per_device, -1)
    received = lax.all_to_all(summed, "mom", split_axis=0, concat_axis=0, tiled=True)
    column = jnp.arange(per_device, dtype=jnp.int32)[:, None]
    source = (cross_map * per_device + column).reshape(-1, 1)
    pick = source == jnp.arange(columns, dtype=jnp.int32)[None, :]
    crossed = jnp.dot(
        pick.astype(BF), received.reshape(columns, -1), preferred_element_type=F32
    )
    return crossed.astype(BF).reshape(per_device, momenta, -1)


def tiled(left_part, vertex, bubble, cross_map):
    momenta = lax.axis_size("mom")
    left, vert = left_part[0], vertex[0]
    rows, half = left.shape
    columns = vert.shape[1]
    per_device = columns // momenta
    square = 2 * columns * half
    unit = rows // 6
    cuts = (0, unit, 3 * unit, 4 * unit, 5 * unit, rows)
    spans = list(zip(cuts, cuts[1:]))

    pieces = fetch(left, spans[:1])
    pieces += fetch(left, spans[1:])
    fars = []
    for piece in pieces:
        fars.append(swap(piece, "col"))
    flipped = local(flip_body, pltpu.VMEM((columns, rows), BF), vert)
    flipped_far = swap(flipped, "row")
    halves, first, other = local(
        near_body,
        [
            pltpu.VMEM((2, rows, half), BF),
            pltpu.VMEM((columns, rows), F32),
            pltpu.VMEM((columns, half), BF),
        ],
        left,
        bubble,
        flipped,
        flipped_far,
        flops=square * rows,
    )
    group = 16 * (2 - per_device // 16 % 2)
    pick = local(
        pick_body(group), pltpu.VMEM((columns, momenta * group), BF), cross_map.T
    )
    order = steps_of(momenta) + [(0, 0)]
    own, others, total = [], [], None
    for i, (s, e) in enumerate(spans):
        extra = []
        if e == rows:
            peeked = local(
                peek_body(order[0], s),
                pltpu.VMEM((per_device, e - s), BF),
                fars[i],
                bubble,
                other,
                first,
                flops=square * (e - s) // momenta,
            )
            ahead = swap(peeked, "row")
            extra = [peeked]
        halves, first, rounded = local(
            chunk_body(s, e),
            [
                pltpu.VMEM((2, rows, half), BF),
                pltpu.VMEM((columns, rows), F32),
                pltpu.VMEM((columns, e - s), BF),
            ],
            fars[i],
            bubble,
            other,
            halves,
            first,
            *extra,
            aliases={3: 0, 4: 1},
            flops=square * (e - s),
        )
        own.append(rounded)
        others.append(swap(rounded, "row"))
        if e == rows:
            break
        inputs = [*own, *others[:i], halves, flipped, first]
        total = local(
            add_body(spans, i),
            pltpu.VMEM((columns, rows), F32),
            *inputs,
            *([] if total is None else [total]),
            aliases={} if total is None else {len(inputs): 0},
            flops=square * 2 * (e - s),
        )
        if i == len(spans) - 2:
            total = local(
                settle_body(spans[i]),
                pltpu.VMEM((columns, rows), F32),
                halves,
                others[i],
                total,
                aliases={2: 0},
                flops=square * (e - s),
            )

    part = local(
        own_body(spans, order[0]),
        pltpu.VMEM((per_device, rows), F32),
        *own,
        *others[:-1],
        halves,
        flipped,
        first,
        total,
        peeked,
        flops=square * unit // momenta,
    )
    sent = [
        local(
            close_body(spans[-1]),
            pltpu.VMEM((per_device, rows), BF),
            halves,
            ahead,
            part,
            flops=square * unit // momenta,
        )
    ]
    for chosen in (order[1:2], order[2:]):
        scratch = [pltpu.VMEM((columns, rows), BF)] if len(chosen) > 2 else []
        sent += local(
            finish_body(spans, chosen),
            [pltpu.VMEM((per_device, rows), BF)] * len(chosen),
            *own,
            *others,
            halves,
            flipped,
            first,
            total,
            flops=square * unit * len(chosen) // momenta,
            scratch=scratch,
        )
    got = []
    for block, step in zip(sent, order[:-1]):
        pairs = [(m, meet(m, step)) for m in range(momenta)]
        got.append(lax.ppermute(block, "mom", pairs))
    arrays = [pick, *got, sent[-1]]
    crossed = pl.pallas_call(
        cross_body(order, group),
        out_shape=jax.ShapeDtypeStruct((columns, rows), BF),
        in_specs=[VMEM] * len(arrays),
        out_specs=ANY,
        scratch_shapes=[
            pltpu.VMEM((per_device // group, momenta * group, rows), BF),
            pltpu.VMEM((columns, rows), BF),
            pltpu.SemaphoreType.DMA((2 * per_device // group,)),
        ],
        compiler_params=LIMIT,
    )(*[pltpu.with_memory_space_constraint(a, pltpu.VMEM) for a in arrays])
    return crossed.reshape(per_device, momenta, rows)


def solution(mesh):
    in_specs = (
        P("mom", "row", "col"),
        P("mom", "row", "col"),
        P("mom", None),
        P(("col", "mom"), None),
    )
    out_specs = P(("col", "mom"), None, "row")

    def step(body):
        return jax.shard_map(
            body, mesh=mesh, in_specs=in_specs, out_specs=out_specs, check_vma=False
        )

    momenta = mesh.shape["mom"]

    def run(left_part, *rest):
        per_device = left_part.shape[1] // momenta
        if per_device % 16 or momenta & (momenta - 1) or momenta < 2:
            return step(plain)(left_part, *rest)
        return step(tiled)(
            left_part, *rest
        )

    return run
```

```python
import jax
import jax.numpy as jnp
from jax import lax
from jax.experimental import pallas as pl
from jax.experimental.pallas import tpu as pltpu
from jax.sharding import PartitionSpec as P


LIMIT = pltpu.CompilerParams(vmem_limit_bytes=16 << 20)
VMEM = pl.BlockSpec(memory_space=pltpu.VMEM)
HBM = pl.BlockSpec(memory_space=pltpu.HBM)
ANY = pl.BlockSpec(memory_space=pl.ANY)
BF, F32 = jnp.bfloat16, jnp.float32
PARTS = (1, 3, 1, 1)


def swap(value, axis):
    return lax.ppermute(value, axis, [(0, 1), (1, 0)])


def nt(x, y):
    return lax.dot_general(
        x, y, (((1,), (1,)), ((), ())), preferred_element_type=F32
    )


def local(body, outs, *arrays, aliases=None, flops=0, scratch=()):
    arrays = [pltpu.with_memory_space_constraint(a, pltpu.VMEM) for a in arrays]
    many = isinstance(outs, list)
    return pl.pallas_call(
        body,
        out_shape=outs,
        in_specs=[VMEM] * len(arrays),
        out_specs=[VMEM] * len(outs) if many else VMEM,
        scratch_shapes=scratch,
        input_output_aliases=aliases or {},
        compiler_params=LIMIT,
        cost_estimate=pl.CostEstimate(
            flops=flops, bytes_accessed=1 << 20, transcendentals=0
        ),
    )(*arrays)


def fetch(array, spans):
    def body(source, *refs):
        outs, sem = refs[:-1], refs[-1]
        copies = [
            pltpu.make_async_copy(source.at[s:e, :], out, sem.at[i])
            for i, (out, (s, e)) in enumerate(zip(outs, spans))
        ]
        for copy in copies:
            copy.start()
        for copy in copies:
            copy.wait()

    return pl.pallas_call(
        body,
        out_shape=[pltpu.VMEM((e - s, array.shape[1]), array.dtype) for s, e in spans],
        in_specs=[HBM],
        out_specs=[VMEM] * len(spans),
        scratch_shapes=[pltpu.SemaphoreType.DMA((len(spans),))],
        compiler_params=LIMIT,
    )(pltpu.with_memory_space_constraint(array, pltpu.HBM))


def flip_body(vert, out):
    out[...] = vert[...].T


def near_body(left, bubble, flipped, flipped_far, halves, first, other):
    row, col = lax.axis_index("row"), lax.axis_index("col")
    half = left.shape[1]
    scale = bubble[:, pl.ds(pl.multiple_of(col * half, half), half)]
    near = (left[...].astype(F32) * scale).astype(BF)
    halves[col] = near

    @pl.when(row == col)
    def _():
        first[...] = nt(flipped[...], near)
        other[...] = flipped_far[...]

    @pl.when(row != col)
    def _():
        first[...] = nt(flipped_far[...], near)
        other[...] = flipped[...]


def chunk_body(start, stop):
    def body(far, bubble, other, *refs):
        halves, first, rounded = refs[-3:]
        col = 1 - lax.axis_index("col")
        half = far.shape[1]
        scale = bubble[:, pl.ds(pl.multiple_of(col * half, half), half)]
        scaled = (far[...].astype(F32) * scale).astype(BF)
        halves[col, start:stop, :] = scaled
        total = first[:, start:stop] + nt(other[...], scaled)
        first[:, start:stop] = total
        rounded[...] = total.astype(BF)

    return body


def add_body(spans, i):
    def body(*refs):
        row = lax.axis_index("row")
        own, refs = refs[: i + 1], refs[i + 1 :]
        far, refs = refs[:i], refs[i:]
        halves, flipped, first, total = refs[0], refs[1], refs[2], refs[-1]
        start, stop = spans[i]
        if i:
            s, e = spans[i - 1]
            part = total[:, :start] + nt(own[i][...], halves[row, :start, start:stop])
            part += nt(far[i - 1][...], halves[1 - row, :start, s:e])
            total[:, :start] = part
        part = flipped[:, start:stop].astype(F32) + first[:, start:stop]
        for half, terms in ((row, own), (1 - row, far)):
            for term, (s, e) in zip(terms, spans):
                part += nt(term[...], halves[half, start:stop, s:e])
        total[:, start:stop] = part

    return body


def settle_body(span):
    def body(halves, far, _, total):
        other = 1 - lax.axis_index("row")
        s, e = span
        total[:, :e] += nt(far[...], halves[other, :e, s:e])

    return body


def peek_body(step, start):
    def body(far, bubble, other, first, out):
        col, mom = 1 - lax.axis_index("col"), lax.axis_index("mom")
        half, size = far.shape[1], out.shape[0]
        scale = bubble[:, pl.ds(pl.multiple_of(col * half, half), half)]
        scaled = (far[...].astype(F32) * scale).astype(BF)
        lines = pl.ds(pl.multiple_of(meet(mom, step) * size, size), size)
        out[...] = (first[lines, start:] + nt(other[lines, :], scaled)).astype(BF)

    return body


def own_body(spans, step):
    def body(*refs):
        row, mom = lax.axis_index("row"), lax.axis_index("mom")
        count = len(spans)
        own, far, refs = refs[:count], refs[count : 2 * count - 1], refs[2 * count - 1 :]
        halves, flipped, first, total, size_like, out = refs
        start, stop = spans[-1]
        size = size_like.shape[0]
        lines = pl.ds(pl.multiple_of(meet(mom, step) * size, size), size)
        out[:, :start] = total[lines, :start] + nt(
            own[-1][lines, :], halves[row, :start, start:stop]
        )
        part = flipped[lines, start:stop].astype(F32) + first[lines, start:stop]
        for half, terms in ((row, own), (1 - row, far)):
            for term, (s, e) in zip(terms, spans):
                part += nt(term[lines, :], halves[half, start:stop, s:e])
        out[:, start:] = part

    return body


def close_body(span):
    def body(halves, last, part, out):
        s, e = span
        weights = halves[1 - lax.axis_index("row"), :, s:e]
        out[...] = (part[...] + nt(last[...], weights)).astype(BF)

    return body


def finish_body(spans, steps):
    def body(*refs):
        row, mom = lax.axis_index("row"), lax.axis_index("mom")
        count = len(spans)
        own, far, refs = refs[:count], refs[count : 2 * count], refs[2 * count :]
        halves, flipped, first, total = refs[:4]
        outs = refs[4:]
        start, stop = spans[-1]
        size = outs[0].shape[0]
        done = None
        if len(steps) > 2:
            outs, done = outs[:-1], outs[-1]
        blocks = [done] if done is not None else outs
        for out, step in zip(blocks, steps):
            begin = 0 if done is not None else meet(mom, step) * size
            lines = pl.ds(pl.multiple_of(begin, size), out.shape[0])
            part = total[lines, :start]
            part += nt(own[-1][lines, :], halves[row, :start, start:stop])
            part += nt(far[-1][lines, :], halves[1 - row, :start, start:stop])
            out[:, :start] = part.astype(BF)
            part = flipped[lines, start:stop].astype(F32) + first[lines, start:stop]
            for half, terms in ((row, own), (1 - row, far)):
                for term, (s, e) in zip(terms, spans):
                    part += nt(term[lines, :], halves[half, start:stop, s:e])
            out[:, start:] = part.astype(BF)
        if done is not None:
            for out, step in zip(outs, steps):
                begin = pl.multiple_of(meet(mom, step) * size, size)
                out[...] = done[pl.ds(begin, size), :]

    return body


def cross_body(steps, group):
    momenta = len(steps)

    def body(pick, *refs):
        blocks, (out, gathered, result, sem) = refs[:momenta], refs[momenta:]
        mom = lax.axis_index("mom")
        groups = out.shape[0] // (momenta * group)
        size = group * momenta
        copies = []
        for i in range(groups):
            for block, step in zip(blocks, steps):
                begin = pl.multiple_of(meet(mom, step) * group, group)
                gathered[i, pl.ds(begin, group), :] = block[
                    i * group : (i + 1) * group, :
                ]
            span = slice(i * size, (i + 1) * size)
            width = out.shape[1] // 2
            for j in range(2):
                lanes = slice(j * width, (j + 1) * width)
                result[span, lanes] = jnp.dot(
                    pick[span, :], gathered[i, :, lanes], preferred_element_type=F32
                ).astype(BF)
                copy = pltpu.make_async_copy(
                    result.at[span, lanes], out.at[span, lanes], sem.at[2 * i + j]
                )
                copy.start()
                copies.append(copy)
        for copy in copies:
            copy.wait()

    return body


def team(mom):
    return ((mom >> 1) ^ (mom >> 2)) & 1


def meet(mom, step):
    outer, inner = step
    return mom ^ (outer + team(mom) * (inner - outer))


def steps_of(momenta):
    def key(k):
        return (-k.bit_length(), int(format(k, "b")[::-1], 2))

    steps = [(k, k) for k in sorted(range(1, momenta), key=key)]
    if momenta >= 8:
        far = momenta - 2
        mixed = [(1, far), (far, 1)]
        steps = [k for k in steps if k[0] not in (1, far)]
        steps = mixed[:1] + [(5, 5), (2, 2), (4, 4), (3, 3)] + mixed[1:] + [(7, 7)]
    return steps


def pick_body(group):
    def body(cross_map, out):
        momenta, per = cross_map.shape
        wide = (momenta * per, per)
        line = lax.broadcasted_iota(jnp.int32, wide, 0) // momenta
        spread = (line == lax.broadcasted_iota(jnp.int32, wide, 1)).astype(BF)
        known = nt(spread, cross_map[...].astype(F32).astype(BF))
        tall = (momenta * per, momenta)
        line = lax.broadcasted_iota(jnp.int32, tall, 0)
        mine = line % momenta == lax.broadcasted_iota(jnp.int32, tall, 1)
        wanted = jnp.sum(jnp.where(mine, known, 0.0), axis=1, keepdims=True)
        column = (line[:, :1] // momenta) % group
        wanted = wanted.astype(jnp.int32) * group + column
        spot = lax.broadcasted_iota(jnp.int32, out.shape, 1)
        out[...] = jnp.where(spot == wanted, 1.0, 0.0).astype(BF)

    return body


def plain(left_part, vertex, bubble, cross_map):
    momenta = lax.axis_size("mom")
    col = lax.axis_index("col")
    same = lax.axis_index("row") == col
    left, flipped = left_part[0], vertex[0].T
    half = left.shape[1]
    columns = flipped.shape[0]
    per_device = columns // momenta

    left_far, flipped_far = swap(left, "col"), swap(flipped, "row")
    scale = bubble.reshape(2, half)
    near_scale = lax.dynamic_index_in_dim(scale, col, 0, keepdims=True)
    far_scale = lax.dynamic_index_in_dim(scale, 1 - col, 0, keepdims=True)
    near = (left.astype(F32) * near_scale).astype(BF)
    far = (left_far.astype(F32) * far_scale).astype(BF)
    first = nt(jnp.where(same, flipped, flipped_far), near)
    first = first + nt(jnp.where(same, flipped_far, flipped), far)
    rounded = first.astype(BF)
    rounded_far = swap(rounded, "row")
    second = nt(jnp.where(same, rounded, rounded_far), near)
    second = second + nt(jnp.where(same, rounded_far, rounded), far)
    summed = (flipped.astype(F32) + first + second).astype(BF)

    summed = summed.reshape(momenta, per_device, -1)
    received = lax.all_to_all(summed, "mom", split_axis=0, concat_axis=0, tiled=True)
    column = jnp.arange(per_device, dtype=jnp.int32)[:, None]
    source = (cross_map * per_device + column).reshape(-1, 1)
    pick = source == jnp.arange(columns, dtype=jnp.int32)[None, :]
    crossed = jnp.dot(
        pick.astype(BF), received.reshape(columns, -1), preferred_element_type=F32
    )
    return crossed.astype(BF).reshape(per_device, momenta, -1)


def tiled(left_part, vertex, bubble, cross_map):
    momenta = lax.axis_size("mom")
    left, vert = left_part[0], vertex[0]
    rows, half = left.shape
    columns = vert.shape[1]
    per_device = columns // momenta
    square = 2 * columns * half
    unit = rows // sum(PARTS)
    cuts = [unit * sum(PARTS[:i]) for i in range(len(PARTS) + 1)]
    spans = list(zip(cuts, cuts[1:]))

    pieces = fetch(left, spans[:1])
    pieces += fetch(left, spans[1:])
    fars = []
    for piece in pieces:
        fars.append(swap(piece, "col"))
    flipped = local(flip_body, pltpu.VMEM((columns, rows), BF), vert)
    flipped_far = swap(flipped, "row")
    halves, first, other = local(
        near_body,
        [
            pltpu.VMEM((2, rows, half), BF),
            pltpu.VMEM((columns, rows), F32),
            pltpu.VMEM((columns, half), BF),
        ],
        left,
        bubble,
        flipped,
        flipped_far,
        flops=square * rows,
    )
    group = 16 * (2 - per_device // 16 % 2)
    pick = local(
        pick_body(group), pltpu.VMEM((columns, momenta * group), BF), cross_map.T
    )
    order = steps_of(momenta) + [(0, 0)]
    own, others, total = [], [], None
    for i, (s, e) in enumerate(spans):
        extra = []
        if e == rows:
            peeked = local(
                peek_body(order[0], s),
                pltpu.VMEM((per_device, e - s), BF),
                fars[i],
                bubble,
                other,
                first,
                flops=square * (e - s) // momenta,
            )
            ahead = swap(peeked, "row")
            extra = [peeked]
        halves, first, rounded = local(
            chunk_body(s, e),
            [
                pltpu.VMEM((2, rows, half), BF),
                pltpu.VMEM((columns, rows), F32),
                pltpu.VMEM((columns, e - s), BF),
            ],
            fars[i],
            bubble,
            other,
            halves,
            first,
            *extra,
            aliases={3: 0, 4: 1},
            flops=square * (e - s),
        )
        own.append(rounded)
        others.append(swap(rounded, "row"))
        if e == rows:
            break
        inputs = [*own, *others[:i], halves, flipped, first]
        total = local(
            add_body(spans, i),
            pltpu.VMEM((columns, rows), F32),
            *inputs,
            *([] if total is None else [total]),
            aliases={} if total is None else {len(inputs): 0},
            flops=square * 2 * (e - s),
        )
        if i == len(spans) - 2:
            total = local(
                settle_body(spans[i]),
                pltpu.VMEM((columns, rows), F32),
                halves,
                others[i],
                total,
                aliases={2: 0},
                flops=square * (e - s),
            )

    part = local(
        own_body(spans, order[0]),
        pltpu.VMEM((per_device, rows), F32),
        *own,
        *others[:-1],
        halves,
        flipped,
        first,
        total,
        peeked,
        flops=square * unit // momenta,
    )
    sent = [
        local(
            close_body(spans[-1]),
            pltpu.VMEM((per_device, rows), BF),
            halves,
            ahead,
            part,
            flops=square * unit // momenta,
        )
    ]
    for chosen in (order[1:2], order[2:]):
        scratch = [pltpu.VMEM((columns, rows), BF)] if len(chosen) > 2 else []
        sent += local(
            finish_body(spans, chosen),
            [pltpu.VMEM((per_device, rows), BF)] * len(chosen),
            *own,
            *others,
            halves,
            flipped,
            first,
            total,
            flops=square * unit * len(chosen) // momenta,
            scratch=scratch,
        )
    got = []
    for block, step in zip(sent, order[:-1]):
        pairs = [(m, meet(m, step)) for m in range(momenta)]
        got.append(lax.ppermute(block, "mom", pairs))
    arrays = [pick, *got, sent[-1]]
    crossed = pl.pallas_call(
        cross_body(order, group),
        out_shape=jax.ShapeDtypeStruct((columns, rows), BF),
        in_specs=[VMEM] * len(arrays),
        out_specs=ANY,
        scratch_shapes=[
            pltpu.VMEM((per_device // group, momenta * group, rows), BF),
            pltpu.VMEM((columns, rows), BF),
            pltpu.SemaphoreType.DMA((2 * per_device // group,)),
        ],
        compiler_params=LIMIT,
    )(*[pltpu.with_memory_space_constraint(a, pltpu.VMEM) for a in arrays])
    return crossed.reshape(per_device, momenta, rows)


def solution(mesh):
    in_specs = (
        P("mom", "row", "col"),
        P("mom", "row", "col"),
        P("mom", None),
        P(("col", "mom"), None),
    )
    out_specs = P(("col", "mom"), None, "row")

    def step(body):
        return jax.shard_map(
            body, mesh=mesh, in_specs=in_specs, out_specs=out_specs, check_vma=False
        )

    momenta = mesh.shape["mom"]

    def run(left_part, *rest):
        rows = left_part.shape[1] // mesh.shape["row"]
        columns = left_part.shape[1] // mesh.shape["col"]
        fits = rows % (128 * sum(PARTS)) == 0 and columns % (16 * momenta) == 0
        if not fits or momenta & (momenta - 1) or momenta < 4:
            return step(plain)(left_part, *rest)
        return step(tiled)(left_part, *rest)

    return run
```
